256 devices in a mesh: wave: 128 (over x, y, z), par: 2 (over core).
Axes of the slice: x: 4, y: 4, z: 8, core: 2. Of those that a mesh axis runs over, the one named last changes fastest.
Arguments:
- fourier: float32 [2, 1024, 128, 256], P('par', 'wave'), may hold values from -6 to 6
- legendre: float32 [128, 2, 2000, 1024], P('wave', 'par'), may hold values from -0.1875 to 0.1875
- window_waves: int32 [128], P('wave'), may hold values from 0 to 3999, as said below
- lat_order: int32 [1024], replicated, may hold values from 0 to 1023, each once
- gauss_weights: float32 [1024], replicated, may hold values from 0.2 to 1
- mode_rates: float32 [128], replicated, may hold values from 0.5 to 20
- mode_in: float32 [128, 128], replicated, may hold values from -0.5 to 0.5
- mode_out: float32 [128, 128], replicated, may hold values from -0.5 to 0.5
Outputs:
- updated: float32 [2, 1024, 128, 256], P('par', 'wave')
The draws below stay inside these ranges and needn't reach their ends.
Inputs may be any that keep to these rules, and one draw needn't show every extreme that they name: `window_waves`: distinct wavenumbers; 0 is always among them.
All inputs are finite; a program needn't handle non-finite values.
Results may differ from the reference program's by a relative error of at most 0.0003.
Values sent between devices are 32-bit elements; how exact they have to be, the bound alone decides.
A program may use at most 64 MiB of HBM per device.

```python
import math
import jax
import jax.numpy as jnp
from jax import lax

TRUNC = 3999
NLAT = 1024
LEV = 128
NDEGP = 2000
WAVES = 128


def draw_window_waves(key, part):
    first_key, second_key = jax.random.split(key)
    others = (jax.random.permutation(first_key, TRUNC) + 1).astype(jnp.int32)
    picked = jnp.concatenate([jnp.zeros((1,), jnp.int32), others[:WAVES - 1]])
    shuffle = jax.random.permutation(second_key, WAVES)
    return picked[shuffle]


def level_of(stream_key, extent, cuts, smallest, high):
    level, own = 1.0, jax.random.fold_in(stream_key, 6)
    for position, shards_of in cuts:
        draws = jnp.exp(jax.random.uniform(jax.random.fold_in(own, position), (shards_of,), jnp.float32, smallest / len(cuts), high / len(cuts)))
        level = level * jnp.repeat(draws, extent[position] // shards_of).reshape([-1 if axis == position else 1 for axis in range(len(extent))])
    return level


def noise(stream_key, extent, spread, bound, cuts=(), held_as=jnp.bfloat16):
    loudness = level_of(stream_key, extent, cuts, -0.22, 0.18) if cuts else 1.0
    drawn = jax.random.normal(stream_key, extent, jnp.float32) * spread * loudness
    return jnp.minimum(jnp.maximum(drawn, -bound), bound).astype(held_as)


def setup_inputs(seed: int = 0) -> dict:
    key_of = jax.random.split(jax.random.key(seed), 9)
    fourier = noise(key_of[0], (2, NLAT, WAVES, 2 * LEV), 1.0, 6.0, ((0, 2), (1, 128)), jnp.float32)
    legendre = noise(key_of[1], (WAVES, 2, NDEGP, NLAT), NLAT ** -0.5, 0.1875, ((0, 128), (1, 2)), jnp.float32)
    window_waves = draw_window_waves(jax.random.fold_in(key_of[8], 71), 0)
    lat_order = jax.random.permutation(key_of[3], NLAT).astype(jnp.int32)
    gauss_weights = jnp.clip(jnp.exp(jax.random.uniform(key_of[4], (NLAT,), jnp.float32, math.log(0.2), math.log(1.0))), 0.2, 1.0)
    mode_rates = jnp.clip(jnp.exp(jax.random.uniform(key_of[5], (LEV,), jnp.float32, math.log(0.5), math.log(20.0))), 0.5, 20.0)
    mode_in = noise(key_of[6], (LEV, LEV), LEV ** -0.5, 0.5, (), jnp.float32)
    mode_out = noise(key_of[7], (LEV, LEV), LEV ** -0.5, 0.5, (), jnp.float32)
    return {"fourier": fourier, "legendre": legendre, "window_waves": window_waves, "lat_order": lat_order, "gauss_weights": gauss_weights, "mode_rates": mode_rates, "mode_in": mode_in, "mode_out": mode_out}


precise = lax.Precision.HIGHEST


def vertical(spectrum, degree, mode_rates, mode_in, mode_out):
    total_rows = spectrum.shape[0]
    levels = mode_in.shape[0]
    flattened = spectrum.reshape(total_rows * 2, levels)
    mode_vals = jnp.dot(flattened, mode_in, precision=precise, preferred_element_type=jnp.float32)
    mode_vals = mode_vals.reshape(total_rows, 2, levels)
    degree_scale = degree * (degree + 1.0) / (TRUNC * (TRUNC + 1.0))
    mode_vals = mode_vals / (1.0 + degree_scale[:, None, None] * mode_rates[None, None, :])
    returned = jnp.dot(mode_vals.reshape(total_rows * 2, levels), mode_out, precision=precise, preferred_element_type=jnp.float32)
    return returned.reshape(total_rows, 2 * levels)


def one_parity(field_rows, table_rows, wavenum, parity, lat_order, gauss_weights, mode_rates, mode_in, mode_out):
    in_lat = jnp.zeros_like(field_rows).at[lat_order].set(field_rows)
    weighted = gauss_weights[:, None] * in_lat
    degree = wavenum + parity + 2 * jnp.arange(table_rows.shape[0], dtype=jnp.int32)
    live_rows = (degree <= TRUNC).astype(jnp.float32)
    spectrum = jnp.dot(table_rows, weighted, precision=precise, preferred_element_type=jnp.float32) * live_rows[:, None]
    solved = vertical(spectrum, degree.astype(jnp.float32), mode_rates, mode_in, mode_out)
    grid_lat = lax.dot_general(table_rows, solved, (((0,), (0,)), ((), ())), precision=precise, preferred_element_type=jnp.float32)
    return jnp.take(grid_lat, lat_order, axis=0)


def reference(fourier, legendre, window_waves, lat_order, gauss_weights, mode_rates, mode_in, mode_out):
    paired = jnp.stack([fourier[0] + fourier[1], fourier[0] - fourier[1]])

    def per_wave(index_wave):
        columns = lax.dynamic_index_in_dim(paired, index_wave, 2, keepdims=False)
        tables = lax.dynamic_index_in_dim(legendre, index_wave, 0, keepdims=False)
        wavenum = window_waves[index_wave]
        even_part = one_parity(columns[0], tables[0], wavenum, 0, lat_order, gauss_weights, mode_rates, mode_in, mode_out)
        odd_part = one_parity(columns[1], tables[1], wavenum, 1, lat_order, gauss_weights, mode_rates, mode_in, mode_out)
        return jnp.stack([even_part + odd_part, even_part - odd_part])

    results = lax.map(per_wave, jnp.arange(WAVES, dtype=jnp.int32))
    return jnp.transpose(results, (1, 2, 0, 3))
```

```python
import functools

import jax
import jax.numpy as jnp
from jax import lax
from jax.experimental import pallas as pl
from jax.experimental.pallas import tpu as pltpu
from jax.sharding import PartitionSpec as P

TRUNC = 3999
LANES = 128
precise = lax.Precision.HIGHEST
MESH = pl.DeviceIdType.MESH
f32, bf16 = jnp.float32, jnp.bfloat16


def at_offset(me, k, n):
    if n != 128:
        return (me + k) % n
    x, y, z = me // 32, (me // 8) % 4, me % 8
    dx, dy, dz = k // 32, (k // 8) % 4, k % 8
    return ((x + dx) % 4) * 32 + ((y + dy) % 4) * 8 + (z + dz) % 8


def split(value):
    high = value.astype(bf16)
    return high, (value - high.astype(f32)).astype(bf16)


def mm(a, b):
    return jnp.dot(a, b, preferred_element_type=f32)


def mm_nt(a, b, precision=None):
    return lax.dot_general(
        a, b, (((1,), (1,)), ((), ())), precision=precision, preferred_element_type=f32
    )


def step_kernel(
    n, wave_ref, field_hbm, table_hbm, order_ref, gauss_ref, rates_ref, in_ref, out_mat_ref,
    result,
    field, table, high, low, pick, place, gauss_col, out_t,
    send, recv, other, stack, weighted, solved_t, grid_t, back, back_other, send_out,
    field_sem, table_sem, in_send, in_recv, pair_send, pair_recv,
    out_send, out_recv, back_send, back_recv, own_sem,
):
    me = lax.axis_index("wave")
    par = lax.axis_index("par")
    lats = 8 * n
    slots = table.shape[0]
    padded = high.shape[0]
    tile = min(256, lats)
    jtile = 256
    sign = (1 - 2 * par).astype(f32)
    partner = {"par": 1 - par}

    barrier = pltpu.get_barrier_semaphore()
    field_in = [
        pltpu.make_async_copy(
            field_hbm.at[:, pl.ds(h * LANES, LANES)], field.at[h], field_sem.at[h]
        )
        for h in range(2)
    ]
    for copy in field_in:
        copy.start()
    table_in = pltpu.make_async_copy(table_hbm, table, table_sem)
    table_in.start()
    pl.semaphore_signal(barrier, inc=1, device_id=partner, device_id_type=MESH)

    @pl.loop(1, n)
    def _(k):
        pl.semaphore_signal(
            barrier, inc=1, device_id={"wave": at_offset(me, k, n)}, device_id_type=MESH
        )

    for h in range(2):
        field_in[h].wait()

        @pl.loop(0, n)
        def _(w, h=h):
            send[h, w] = field[h, pl.ds(w, 8, stride=n), :]

        recv[h, pl.ds(me, 1)] = send[h, pl.ds(me, 1)]

    pl.semaphore_wait(barrier, n)

    def send_all(source, target, send_sem, recv_sem, h):
        @pl.loop(1, n)
        def _(k):
            d = at_offset(me, k, n)
            pltpu.make_async_remote_copy(
                src_ref=source.at[h, d],
                dst_ref=target.at[h, me],
                send_sem=send_sem.at[h],
                recv_sem=recv_sem.at[h],
                device_id={"wave": d},
                device_id_type=MESH,
            ).start()

    def all_of(source, target, send_sem, recv_sem, h):
        return pltpu.make_async_remote_copy(
            src_ref=source.at[h, pl.ds(0, n - 1)],
            dst_ref=target.at[h, pl.ds(0, n - 1)],
            send_sem=send_sem.at[h],
            recv_sem=recv_sem.at[h],
            device_id=partner,
            device_id_type=MESH,
        )

    for h in range(2):
        send_all(send, recv, in_send, in_recv, h)

    for t in range(lats // LANES):
        rows = pl.ds(t * LANES, LANES)
        gauss_col[rows, :] = jnp.broadcast_to(gauss_ref[t : t + 1, :], (LANES, LANES)).T
        order_t = jnp.broadcast_to(order_ref[t : t + 1, :].astype(f32), (LANES, LANES)).T
        order_t = order_t.astype(jnp.int32)
        for c in range(lats // LANES):
            lat = lax.broadcasted_iota(jnp.int32, (LANES, LANES), 1) + c * LANES
            pick[rows, pl.ds(c * LANES, LANES)] = jnp.where(order_t == lat, 1.0, 0.0).astype(bf16)

    @pl.loop(0, lats // LANES)
    def _(c):
        lat = lax.broadcasted_iota(jnp.int32, (LANES, LANES), 0) + c * LANES
        for t in range(lats // LANES):
            same = order_ref[t : t + 1, :] == lat
            place[pl.ds(pl.multiple_of(c * LANES, LANES), LANES), pl.ds(t * LANES, LANES)] = (
                jnp.where(same, 1.0, 0.0).astype(bf16)
            )

    out_t[...] = out_mat_ref[...].T
    table_in.wait()

    @pl.loop(0, slots // 16)
    def _(c):
        rows = pl.ds(pl.multiple_of(c * 16, 16), 16)
        high[rows, :], low[rows, :] = split(table[rows, :])

    rest = padded - slots
    high[pl.ds(slots, rest), :] = jnp.zeros((rest, lats), bf16)
    low[pl.ds(slots, rest), :] = jnp.zeros((rest, lats), bf16)

    @pl.loop(0, 2)
    def _(h):
        all_of(send, recv, in_send, in_recv, h).wait_recv()
        pair = pltpu.make_async_remote_copy(
            src_ref=recv.at[h], dst_ref=other.at[h], send_sem=pair_send.at[h],
            recv_sem=pair_recv.at[h], device_id=partner, device_id_type=MESH,
        )
        pair.start()
        pair.wait()

        @pl.loop(0, lats // tile)
        def _(t):
            blocks = pl.ds(t * (tile // 8), tile // 8)
            paired = other[h, blocks] + sign * recv[h, blocks]
            rows = pl.ds(pl.multiple_of(t * tile, tile), tile)
            stack[rows, :LANES], stack[rows, LANES:] = split(paired.reshape(tile, LANES))

        @pl.loop(0, lats // tile)
        def _(t):
            rows = pl.ds(pl.multiple_of(t * tile, tile), tile)
            both = mm(place[rows, :], stack[...])
            scaled = (both[:, :LANES] + both[:, LANES:]) * gauss_col[rows, :]
            weighted[rows, :LANES], weighted[rows, LANES:] = split(scaled)

        @pl.loop(0, padded // jtile)
        def _(t):
            rows = pl.ds(pl.multiple_of(t * jtile, jtile), jtile)
            both = mm(high[rows, :], weighted[...])
            summed = both[:, :LANES] + both[:, LANES:] + mm(low[rows, :], weighted[:, :LANES])
            slot = lax.broadcasted_iota(jnp.int32, (jtile, LANES), 0) + t * jtile
            degree = wave_ref[0] + par + 2 * slot
            spectrum = jnp.where(degree <= TRUNC, summed, 0.0)
            modes = jnp.dot(spectrum, in_ref[...], precision=precise, preferred_element_type=f32)
            degree = degree.astype(f32)
            scale = degree * (degree + 1.0) / (TRUNC * (TRUNC + 1.0))
            modes = modes / (1.0 + scale * rates_ref[...])
            solved = mm_nt(out_t[...], modes, precise)
            solved_t[:LANES, rows], solved_t[LANES:, rows] = split(solved)

        @pl.loop(0, lats // tile)
        def _(t):
            cols = pl.ds(pl.multiple_of(t * tile, tile), tile)
            both = mm(solved_t[...], high[:, cols])
            grid = both[:LANES] + both[LANES:] + mm(solved_t[:LANES, :], low[:, cols])
            grid_t[:LANES, cols], grid_t[LANES:, cols] = split(grid)

        @pl.loop(0, lats // tile)
        def _(t):
            rows = pl.ds(pl.multiple_of(t * tile, tile), tile)
            both = mm_nt(pick[rows, :], grid_t[...])
            back[h, pl.ds(t * (tile // 8), tile // 8)] = (
                both[:, :LANES] + both[:, LANES:]
            ).reshape(tile // 8, 8, LANES)

        swap = pltpu.make_async_remote_copy(
            src_ref=back.at[h], dst_ref=back_other.at[h], send_sem=back_send.at[h],
            recv_sem=back_recv.at[h], device_id=partner, device_id_type=MESH,
        )
        swap.start()
        swap.wait()

        @pl.loop(0, n // 8)
        def _(t):
            blocks = pl.ds(t * 8, 8)
            send_out[h, blocks] = back_other[h, blocks] + sign * back[h, blocks]

        send_all(send_out, result, out_send, out_recv, h)
        pltpu.make_async_copy(send_out.at[h, me], result.at[h, me], own_sem.at[h]).start()

    for h in range(2):
        pltpu.make_async_copy(send_out.at[h, me], result.at[h, me], own_sem.at[h]).wait()
        all_of(send, recv, in_send, in_recv, h).wait_send()
        all_of(send_out, result, out_send, out_recv, h).wait()


def per_device(
    fourier, legendre, window_waves, lat_order, gauss_weights, mode_rates, mode_in, mode_out
):
    n = lax.axis_size("wave")
    lats = gauss_weights.shape[0]
    slots = legendre.shape[2]
    padded = -(-slots // 256) * 256
    vmem = pl.BlockSpec(memory_space=pltpu.VMEM)
    anywhere = pl.BlockSpec(memory_space=pl.ANY)
    blocks = pltpu.VMEM((2, n, 8, LANES), f32)
    dma2 = pltpu.SemaphoreType.DMA((2,))
    flops = 24 * slots * lats * LANES
    out = pl.pallas_call(
        functools.partial(step_kernel, n),
        out_shape=jax.ShapeDtypeStruct((2, n, 8, LANES), f32),
        in_specs=[pl.BlockSpec(memory_space=pltpu.SMEM), anywhere, anywhere] + [vmem] * 5,
        out_specs=anywhere,
        scratch_shapes=[
            pltpu.VMEM((2, lats, LANES), f32),
            pltpu.VMEM((slots, lats), f32),
            pltpu.VMEM((padded, lats), bf16),
            pltpu.VMEM((padded, lats), bf16),
            pltpu.VMEM((lats, lats), bf16),
            pltpu.VMEM((lats, lats), bf16),
            pltpu.VMEM((lats, LANES), f32),
            pltpu.VMEM((LANES, LANES), f32),
            blocks,
            blocks,
            blocks,
            pltpu.VMEM((lats, 2 * LANES), bf16),
            pltpu.VMEM((lats, 2 * LANES), bf16),
            pltpu.VMEM((2 * LANES, padded), bf16),
            pltpu.VMEM((2 * LANES, lats), bf16),
            blocks,
            blocks,
            blocks,
            dma2,
            pltpu.SemaphoreType.DMA,
        ]
        + [dma2] * 9,
        compiler_params=pltpu.CompilerParams(
            collective_id=0, has_side_effects=True, vmem_limit_bytes=56 << 20
        ),
        cost_estimate=pl.CostEstimate(
            flops=flops, bytes_accessed=slots * lats * 4, transcendentals=0
        ),
        name="spectral_step",
    )(
        window_waves,
        fourier.reshape(8 * n, 2 * LANES),
        legendre[0, 0],
        lat_order.reshape(lats // LANES, LANES),
        gauss_weights.reshape(lats // LANES, LANES),
        mode_rates.reshape(1, LANES),
        mode_in,
        mode_out,
    )
    return out.transpose(2, 1, 0, 3).reshape(1, 8, n, 2 * LANES)


def solution(mesh):
    return jax.shard_map(
        per_device,
        mesh=mesh,
        in_specs=(
            P("par", "wave", None, None),
            P("wave", "par", None, None),
            P("wave"),
            P(),
            P(),
            P(),
            P(),
            P(),
        ),
        out_specs=P("par", "wave", None, None),
        check_vma=False,
    )
```

```python
import functools

import jax
import jax.numpy as jnp
from jax import lax
from jax.experimental import pallas as pl
from jax.experimental.pallas import tpu as pltpu
from jax.sharding import PartitionSpec as P

TRUNC = 3999
LANES = 128
MESH = pl.DeviceIdType.MESH
f32, bf16 = jnp.float32, jnp.bfloat16


def at_offset(me, k, n):
    if n != 128:
        return (me + k) % n
    x, y, z = me // 32, (me // 8) % 4, me % 8
    dx, dy, dz = k // 32, (k // 8) % 4, k % 8
    return ((x + dx) % 4) * 32 + ((y + dy) % 4) * 8 + (z + dz) % 8


def split(value):
    high = value.astype(bf16)
    return high, (value - high.astype(f32)).astype(bf16)


def mm(a, b):
    return jnp.dot(a, b, preferred_element_type=f32)


def mm_nt(a, b):
    return lax.dot_general(a, b, (((1,), (1,)), ((), ())), preferred_element_type=f32)


def step_kernel(
    n, wave_ref, field_hbm, table_hbm, order_ref, gauss_ref, rates_ref, in_ref, out_mat_ref,
    result,
    field, table, high, low, pick, place, gauss_col, in_terms, out_terms,
    send, recv, other, stack, weighted, terms, solved_t, grid_t, back, back_other, send_out,
    field_sem, table_sem, in_send, in_recv, pair_send, pair_recv,
    out_send, out_recv, back_send, back_recv, own_sem,
):
    me = lax.axis_index("wave")
    par = lax.axis_index("par")
    lats = 8 * n
    slots = table.shape[0]
    padded = high.shape[0]
    tile = min(256, lats)
    jtile, vtile, ctile, ltile = min(1024, padded), min(1024, padded), min(512, lats), min(1024, lats)
    sign = (1 - 2 * par).astype(f32)
    partner = {"par": 1 - par}

    barrier = pltpu.get_barrier_semaphore()
    field_in = [
        pltpu.make_async_copy(
            field_hbm.at[:, pl.ds(h * LANES, LANES)], field.at[h], field_sem.at[h]
        )
        for h in range(2)
    ]
    for copy in field_in:
        copy.start()
    table_in = pltpu.make_async_copy(table_hbm, table, table_sem)
    table_in.start()
    pl.semaphore_signal(barrier, inc=1, device_id=partner, device_id_type=MESH)

    @pl.loop(1, n)
    def _(k):
        pl.semaphore_signal(
            barrier, inc=1, device_id={"wave": at_offset(me, k, n)}, device_id_type=MESH
        )

    for h in range(2):
        field_in[h].wait()

        @pl.loop(0, n)
        def _(w, h=h):
            send[h, w] = field[h, pl.ds(w, 8, stride=n), :]

        recv[h, pl.ds(me, 1)] = send[h, pl.ds(me, 1)]

    pl.semaphore_wait(barrier, n)

    def send_all(source, target, send_sem, recv_sem, h):
        @pl.loop(1, n)
        def _(k):
            d = at_offset(me, k, n)
            pltpu.make_async_remote_copy(
                src_ref=source.at[h, d],
                dst_ref=target.at[h, me],
                send_sem=send_sem.at[h],
                recv_sem=recv_sem.at[h],
                device_id={"wave": d},
                device_id_type=MESH,
            ).start()

    def all_of(source, target, send_sem, recv_sem, h):
        return pltpu.make_async_remote_copy(
            src_ref=source.at[h, pl.ds(0, n - 1)],
            dst_ref=target.at[h, pl.ds(0, n - 1)],
            send_sem=send_sem.at[h],
            recv_sem=recv_sem.at[h],
            device_id=partner,
            device_id_type=MESH,
        )

    for h in range(2):
        send_all(send, recv, in_send, in_recv, h)

    for t in range(lats // LANES):
        rows = pl.ds(t * LANES, LANES)
        gauss_col[rows, :] = jnp.broadcast_to(gauss_ref[t : t + 1, :], (LANES, LANES)).T
        order_t = jnp.broadcast_to(order_ref[t : t + 1, :].astype(f32), (LANES, LANES)).T
        order_t = order_t.astype(jnp.int32)
        for c in range(lats // LANES):
            lat = lax.broadcasted_iota(jnp.int32, (LANES, LANES), 1) + c * LANES
            pick[rows, pl.ds(c * LANES, LANES)] = jnp.where(order_t == lat, 1.0, 0.0).astype(bf16)

    @pl.loop(0, lats // LANES)
    def _(c):
        lat = lax.broadcasted_iota(jnp.int32, (LANES, LANES), 0) + c * LANES
        for t in range(lats // LANES):
            same = order_ref[t : t + 1, :] == lat
            place[pl.ds(pl.multiple_of(c * LANES, LANES), LANES), pl.ds(t * LANES, LANES)] = (
                jnp.where(same, 1.0, 0.0).astype(bf16)
            )

    in_high, in_low = split(in_ref[...])
    in_terms[:LANES, :LANES], in_terms[:LANES, LANES:] = in_high, in_low
    in_terms[LANES:, :LANES], in_terms[LANES:, LANES:] = in_high, jnp.zeros_like(in_low)
    out_high, out_low = split(out_mat_ref[...].T)
    out_terms[:LANES, :LANES], out_terms[:LANES, LANES:] = out_high, out_high
    out_terms[LANES:, :LANES], out_terms[LANES:, LANES:] = out_low, jnp.zeros_like(out_low)
    table_in.wait()

    @pl.loop(0, slots // 16)
    def _(c):
        rows = pl.ds(pl.multiple_of(c * 16, 16), 16)
        high[rows, :], low[rows, :] = split(table[rows, :])

    rest = padded - slots
    high[pl.ds(slots, rest), :] = jnp.zeros((rest, lats), bf16)
    low[pl.ds(slots, rest), :] = jnp.zeros((rest, lats), bf16)

    def pair_of(h):
        return pltpu.make_async_remote_copy(
            src_ref=recv.at[h], dst_ref=other.at[h], send_sem=pair_send.at[h],
            recv_sem=pair_recv.at[h], device_id=partner, device_id_type=MESH,
        )

    def swap_of(h, t):
        blocks = pl.ds(t * (tile // 8), tile // 8)
        return pltpu.make_async_remote_copy(
            src_ref=back.at[h, blocks], dst_ref=back_other.at[h, blocks],
            send_sem=back_send.at[h, t], recv_sem=back_recv.at[h, t],
            device_id=partner, device_id_type=MESH,
        )

    def solve(h):
        @pl.loop(0, lats // tile)
        def _(t):
            blocks = pl.ds(t * (tile // 8), tile // 8)
            paired = other[h, blocks] + sign * recv[h, blocks]
            rows = pl.ds(pl.multiple_of(t * tile, tile), tile)
            stack[rows, :LANES], stack[rows, LANES:] = split(paired.reshape(tile, LANES))

        for t in range(lats // ltile):
            rows = pl.ds(t * ltile, ltile)
            both = mm(place[rows, :], stack[...])
            scaled = (both[:, :LANES] + both[:, LANES:]) * gauss_col[rows, :]
            weighted[rows, :LANES], weighted[rows, LANES:] = split(scaled)

        @pl.loop(0, padded // jtile)
        def _(t):
            rows = pl.ds(pl.multiple_of(t * jtile, jtile), jtile)
            both = mm(high[rows, :], weighted[...])
            summed = both[:, :LANES] + both[:, LANES:] + mm(low[rows, :], weighted[:, :LANES])
            slot = lax.broadcasted_iota(jnp.int32, (jtile, LANES), 0) + t * jtile
            degree = wave_ref[0] + par + 2 * slot
            spectrum = jnp.where(degree <= TRUNC, summed, 0.0)
            terms[rows, :LANES], terms[rows, LANES:] = split(spectrum)

        @pl.loop(0, padded // vtile)
        def _(t):
            rows = pl.ds(pl.multiple_of(t * vtile, vtile), vtile)
            slot = lax.broadcasted_iota(jnp.int32, (vtile, LANES), 0) + t * vtile
            degree = (wave_ref[0] + par + 2 * slot).astype(f32)
            both = mm(terms[rows, :], in_terms[...])
            scale = degree * (degree + 1.0) / (TRUNC * (TRUNC + 1.0))
            modes = (both[:, :LANES] + both[:, LANES:]) / (1.0 + scale * rates_ref[...])
            modes = jnp.concatenate(split(modes), axis=1)
            both = mm_nt(out_terms[...], modes)
            solved_t[:LANES, rows], solved_t[LANES:, rows] = split(both[:LANES] + both[LANES:])

        @pl.loop(0, lats // ctile)
        def _(t):
            cols = pl.ds(pl.multiple_of(t * ctile, ctile), ctile)
            both = mm(solved_t[...], high[:, cols])
            grid = both[:LANES] + both[LANES:] + mm(solved_t[:LANES, :], low[:, cols])
            grid_t[:LANES, cols], grid_t[LANES:, cols] = split(grid)

        for t in range(lats // tile):
            both = mm_nt(pick[pl.ds(t * tile, tile), :], grid_t[...])
            back[h, pl.ds(t * (tile // 8), tile // 8)] = (
                both[:, :LANES] + both[:, LANES:]
            ).reshape(tile // 8, 8, LANES)
            swap_of(h, t).start()

    def send_back(h):
        for t in range(lats // tile):
            swap_of(h, t).wait()
            blocks = pl.ds(t * (tile // 8), tile // 8)
            send_out[h, blocks] = back_other[h, blocks] + sign * back[h, blocks]
        send_all(send_out, result, out_send, out_recv, h)
        own_out(h).start()

    def own_out(h):
        return pltpu.make_async_copy(send_out.at[h, me], result.at[h, me], own_sem.at[h])

    all_of(send, recv, in_send, in_recv, 0).wait_recv()
    pair_of(0).start()
    pair_of(0).wait()
    solve(0)
    send_back(0)
    all_of(send, recv, in_send, in_recv, 1).wait_recv()
    pair_of(1).start()
    pair_of(1).wait()
    solve(1)
    send_back(1)

    for h in range(2):
        own_out(h).wait()
        all_of(send, recv, in_send, in_recv, h).wait_send()
        all_of(send_out, result, out_send, out_recv, h).wait()


def per_device(
    fourier, legendre, window_waves, lat_order, gauss_weights, mode_rates, mode_in, mode_out
):
    n = lax.axis_size("wave")
    lats = gauss_weights.shape[0]
    slots = legendre.shape[2]
    padded = -(-slots // 256) * 256
    vmem = pl.BlockSpec(memory_space=pltpu.VMEM)
    anywhere = pl.BlockSpec(memory_space=pl.ANY)
    blocks = pltpu.VMEM((2, n, 8, LANES), f32)
    dma2 = pltpu.SemaphoreType.DMA((2,))
    flops = 24 * slots * lats * LANES
    out = pl.pallas_call(
        functools.partial(step_kernel, n),
        out_shape=jax.ShapeDtypeStruct((2, n, 8, LANES), f32),
        in_specs=[pl.BlockSpec(memory_space=pltpu.SMEM), anywhere, anywhere] + [vmem] * 5,
        out_specs=anywhere,
        scratch_shapes=[
            pltpu.VMEM((2, lats, LANES), f32),
            pltpu.VMEM((slots, lats), f32),
            pltpu.VMEM((padded, lats), bf16),
            pltpu.VMEM((padded, lats), bf16),
            pltpu.VMEM((lats, lats), bf16),
            pltpu.VMEM((lats, lats), bf16),
            pltpu.VMEM((lats, LANES), f32),
            pltpu.VMEM((2 * LANES, 2 * LANES), bf16),
            pltpu.VMEM((2 * LANES, 2 * LANES), bf16),
            blocks,
            blocks,
            blocks,
            pltpu.VMEM((lats, 2 * LANES), bf16),
            pltpu.VMEM((lats, 2 * LANES), bf16),
            pltpu.VMEM((padded, 2 * LANES), bf16),
            pltpu.VMEM((2 * LANES, padded), bf16),
            pltpu.VMEM((2 * LANES, lats), bf16),
            blocks,
            blocks,
            blocks,
            dma2,
            pltpu.SemaphoreType.DMA,
        ]
        + [dma2] * 6
        + [pltpu.SemaphoreType.DMA((2, 4))] * 2
        + [dma2],
        compiler_params=pltpu.CompilerParams(
            collective_id=0, has_side_effects=True, vmem_limit_bytes=56 << 20
        ),
        cost_estimate=pl.CostEstimate(
            flops=flops, bytes_accessed=slots * lats * 4, transcendentals=0
        ),
        name="spectral_step",
    )(
        window_waves,
        fourier.reshape(8 * n, 2 * LANES),
        legendre[0, 0],
        lat_order.reshape(lats // LANES, LANES),
        gauss_weights.reshape(lats // LANES, LANES),
        mode_rates.reshape(1, LANES),
        mode_in,
        mode_out,
    )
    return out.transpose(2, 1, 0, 3).reshape(1, 8, n, 2 * LANES)


def solution(mesh):
    return jax.shard_map(
        per_device,
        mesh=mesh,
        in_specs=(
            P("par", "wave", None, None),
            P("wave", "par", None, None),
            P("wave"),
            P(),
            P(),
            P(),
            P(),
            P(),
        ),
        out_specs=P("par", "wave", None, None),
        check_vma=False,
    )
```

```python
import functools

import jax
import jax.numpy as jnp
from jax import lax
from jax.experimental import pallas as pl
from jax.experimental.pallas import tpu as pltpu
from jax.sharding import PartitionSpec as P

TRUNC = 3999
LANES = 128
MESH = pl.DeviceIdType.MESH
f32, bf16 = jnp.float32, jnp.bfloat16


def each_peer(me, n, visit):
    group, z = lax.div(me, 8), lax.rem(me, 8)
    near = [z] + [lax.rem(z + dz, 8) for dz in range(1, 8)]
    for dz in range(1, 8):
        visit(group * 8 + near[dz])

    @pl.loop(1, n // 8)
    def _(g):
        if n == 128:
            x, y = lax.div(group, 4), lax.rem(group, 4)
            there = lax.rem(x + lax.div(g, 4), 4) * 4 + lax.rem(y + lax.rem(g, 4), 4)
        else:
            there = lax.rem(group + g, n // 8)
        for dz in range(8):
            visit(there * 8 + near[dz])


def split(value):
    high = value.astype(bf16)
    return high, (value - high.astype(f32)).astype(bf16)


def mm(a, b):
    return jnp.dot(a, b, preferred_element_type=f32)


def mm_nt(a, b):
    return lax.dot_general(a, b, (((1,), (1,)), ((), ())), preferred_element_type=f32)


def step_kernel(
    n, wave_ref, field_hbm, table_hbm, order_ref, gauss_ref, rates_ref, in_ref, out_mat_ref,
    result,
    field, table, high, low, pick, place, gauss_col, in_terms, out_terms,
    send, recv, other, stack, weighted, terms, solved_t, grid_t, back, back_other, send_out,
    field_sem, table_sem, in_send, in_recv, pair_send, pair_recv,
    out_send, out_recv, back_send, back_recv, own_sem,
):
    me = lax.axis_index("wave")
    par = lax.axis_index("par")
    lats = 8 * n
    slots = table.shape[0]
    padded = high.shape[0]
    tile = min(256, lats)
    jtile, vtile, ctile, ltile = min(1024, padded), min(1024, padded), min(512, lats), min(1024, lats)
    sign = (1 - 2 * par).astype(f32)
    partner = {"par": 1 - par}

    barrier = pltpu.get_barrier_semaphore()
    field_in = [
        pltpu.make_async_copy(
            field_hbm.at[:, pl.ds(h * LANES, LANES)], field.at[h], field_sem.at[h]
        )
        for h in range(2)
    ]
    for copy in field_in:
        copy.start()
    table_in = pltpu.make_async_copy(table_hbm, table, table_sem)
    table_in.start()
    pl.semaphore_signal(barrier, inc=1, device_id=partner, device_id_type=MESH)

    def greet(d):
        pl.semaphore_signal(barrier, inc=1, device_id={"wave": d}, device_id_type=MESH)

    each_peer(me, n, greet)

    for h in range(2):
        field_in[h].wait()

        @pl.loop(0, n, unroll=8)
        def _(w, h=h):
            send[h, w] = field[h, pl.ds(w, 8, stride=n), :]

        recv[h, pl.ds(me, 1)] = send[h, pl.ds(me, 1)]

    pl.semaphore_wait(barrier, n)

    def send_all(source, target, send_sem, recv_sem, h):
        def send_to(d):
            pltpu.make_async_remote_copy(
                src_ref=source.at[h, d],
                dst_ref=target.at[h, me],
                send_sem=send_sem.at[h],
                recv_sem=recv_sem.at[h],
                device_id={"wave": d},
                device_id_type=MESH,
            ).start()

        each_peer(me, n, send_to)

    def all_of(source, target, send_sem, recv_sem, h):
        return pltpu.make_async_remote_copy(
            src_ref=source.at[h, pl.ds(0, n - 1)],
            dst_ref=target.at[h, pl.ds(0, n - 1)],
            send_sem=send_sem.at[h],
            recv_sem=recv_sem.at[h],
            device_id=partner,
            device_id_type=MESH,
        )

    for h in range(2):
        send_all(send, recv, in_send, in_recv, h)

    for t in range(lats // LANES):
        rows = pl.ds(t * LANES, LANES)
        gauss_col[rows, :] = jnp.broadcast_to(gauss_ref[t : t + 1, :], (LANES, LANES)).T
        order_t = jnp.broadcast_to(order_ref[t : t + 1, :].astype(f32), (LANES, LANES)).T
        order_t = order_t.astype(jnp.int32)
        for c in range(lats // LANES):
            lat = lax.broadcasted_iota(jnp.int32, (LANES, LANES), 1) + c * LANES
            pick[rows, pl.ds(c * LANES, LANES)] = jnp.where(order_t == lat, 1.0, 0.0).astype(bf16)

    @pl.loop(0, lats // LANES)
    def _(c):
        lat = lax.broadcasted_iota(jnp.int32, (LANES, LANES), 0) + c * LANES
        for t in range(lats // LANES):
            same = order_ref[t : t + 1, :] == lat
            place[pl.ds(pl.multiple_of(c * LANES, LANES), LANES), pl.ds(t * LANES, LANES)] = (
                jnp.where(same, 1.0, 0.0).astype(bf16)
            )

    in_high, in_low = split(in_ref[...])
    in_terms[:LANES, :LANES], in_terms[:LANES, LANES:] = in_high, in_low
    in_terms[LANES:, :LANES], in_terms[LANES:, LANES:] = in_high, jnp.zeros_like(in_low)
    out_high, out_low = split(out_mat_ref[...].T)
    out_terms[:LANES, :LANES], out_terms[:LANES, LANES:] = out_high, out_high
    out_terms[LANES:, :LANES], out_terms[LANES:, LANES:] = out_low, jnp.zeros_like(out_low)
    table_in.wait()

    @pl.loop(0, slots // 16)
    def _(c):
        rows = pl.ds(pl.multiple_of(c * 16, 16), 16)
        high[rows, :], low[rows, :] = split(table[rows, :])

    rest = padded - slots
    high[pl.ds(slots, rest), :] = jnp.zeros((rest, lats), bf16)
    low[pl.ds(slots, rest), :] = jnp.zeros((rest, lats), bf16)

    def pair_of(h):
        return pltpu.make_async_remote_copy(
            src_ref=recv.at[h], dst_ref=other.at[h], send_sem=pair_send.at[h],
            recv_sem=pair_recv.at[h], device_id=partner, device_id_type=MESH,
        )

    def swap_of(h, t):
        blocks = pl.ds(t * (tile // 8), tile // 8)
        return pltpu.make_async_remote_copy(
            src_ref=back.at[h, blocks], dst_ref=back_other.at[h, blocks],
            send_sem=back_send.at[h, t], recv_sem=back_recv.at[h, t],
            device_id=partner, device_id_type=MESH,
        )

    def solve(h):
        @pl.loop(0, lats // tile)
        def _(t):
            blocks = pl.ds(t * (tile // 8), tile // 8)
            paired = other[h, blocks] + sign * recv[h, blocks]
            rows = pl.ds(pl.multiple_of(t * tile, tile), tile)
            stack[rows, :LANES], stack[rows, LANES:] = split(paired.reshape(tile, LANES))

        for t in range(lats // ltile):
            rows = pl.ds(t * ltile, ltile)
            both = mm(place[rows, :], stack[...])
            scaled = (both[:, :LANES] + both[:, LANES:]) * gauss_col[rows, :]
            weighted[rows, :LANES], weighted[rows, LANES:] = split(scaled)

        @pl.loop(0, padded // jtile)
        def _(t):
            rows = pl.ds(pl.multiple_of(t * jtile, jtile), jtile)
            both = mm(high[rows, :], weighted[...])
            summed = both[:, :LANES] + both[:, LANES:] + mm(low[rows, :], weighted[:, :LANES])
            slot = lax.broadcasted_iota(jnp.int32, (jtile, LANES), 0) + t * jtile
            degree = wave_ref[0] + par + 2 * slot
            spectrum = jnp.where(degree <= TRUNC, summed, 0.0)
            terms[rows, :LANES], terms[rows, LANES:] = split(spectrum)

        @pl.loop(0, padded // vtile)
        def _(t):
            rows = pl.ds(pl.multiple_of(t * vtile, vtile), vtile)
            slot = lax.broadcasted_iota(jnp.int32, (vtile, LANES), 0) + t * vtile
            degree = (wave_ref[0] + par + 2 * slot).astype(f32)
            both = mm(terms[rows, :], in_terms[...])
            scale = degree * (degree + 1.0) / (TRUNC * (TRUNC + 1.0))
            modes = (both[:, :LANES] + both[:, LANES:]) / (1.0 + scale * rates_ref[...])
            modes = jnp.concatenate(split(modes), axis=1)
            both = mm_nt(out_terms[...], modes)
            solved_t[:LANES, rows], solved_t[LANES:, rows] = split(both[:LANES] + both[LANES:])

        @pl.loop(0, lats // ctile)
        def _(t):
            cols = pl.ds(pl.multiple_of(t * ctile, ctile), ctile)
            both = mm(solved_t[...], high[:, cols])
            grid = both[:LANES] + both[LANES:] + mm(solved_t[:LANES, :], low[:, cols])
            grid_t[:LANES, cols], grid_t[LANES:, cols] = split(grid)

        for t in range(lats // tile):
            both = mm_nt(pick[pl.ds(t * tile, tile), :], grid_t[...])
            back[h, pl.ds(t * (tile // 8), tile // 8)] = (
                both[:, :LANES] + both[:, LANES:]
            ).reshape(tile // 8, 8, LANES)
            swap_of(h, t).start()

    def send_back(h):
        for t in range(lats // tile):
            swap_of(h, t).wait()
            blocks = pl.ds(t * (tile // 8), tile // 8)
            send_out[h, blocks] = back_other[h, blocks] + sign * back[h, blocks]
        send_all(send_out, result, out_send, out_recv, h)
        own_out(h).start()

    def own_out(h):
        return pltpu.make_async_copy(send_out.at[h, me], result.at[h, me], own_sem.at[h])

    all_of(send, recv, in_send, in_recv, 0).wait_recv()
    pair_of(0).start()
    pair_of(0).wait()
    solve(0)
    send_back(0)
    all_of(send, recv, in_send, in_recv, 1).wait_recv()
    pair_of(1).start()
    pair_of(1).wait()
    solve(1)
    send_back(1)

    for h in range(2):
        own_out(h).wait()
        all_of(send, recv, in_send, in_recv, h).wait_send()
        all_of(send_out, result, out_send, out_recv, h).wait()


def row_kernel(n, columns_ref, rows_ref):
    for h in range(2):

        @pl.loop(0, n // 8, unroll=True)
        def _(t):
            for r in range(8):
                rows = columns_ref[h, pl.ds(t * 64 + r, 8, stride=8), :]
                rows_ref[pl.ds(r * n + t * 8, 8), pl.ds(h * LANES, LANES)] = rows


def per_device(
    fourier, legendre, window_waves, lat_order, gauss_weights, mode_rates, mode_in, mode_out
):
    n = lax.axis_size("wave")
    lats = gauss_weights.shape[0]
    slots = legendre.shape[2]
    padded = -(-slots // 256) * 256
    vmem = pl.BlockSpec(memory_space=pltpu.VMEM)
    anywhere = pl.BlockSpec(memory_space=pl.ANY)
    blocks = pltpu.VMEM((2, n, 8, LANES), f32)
    dma2 = pltpu.SemaphoreType.DMA((2,))
    flops = 24 * slots * lats * LANES
    out = pl.pallas_call(
        functools.partial(step_kernel, n),
        out_shape=jax.ShapeDtypeStruct((2, n, 8, LANES), f32),
        in_specs=[pl.BlockSpec(memory_space=pltpu.SMEM), anywhere, anywhere] + [vmem] * 5,
        out_specs=anywhere,
        scratch_shapes=[
            pltpu.VMEM((2, lats, LANES), f32),
            pltpu.VMEM((slots, lats), f32),
            pltpu.VMEM((padded, lats), bf16),
            pltpu.VMEM((padded, lats), bf16),
            pltpu.VMEM((lats, lats), bf16),
            pltpu.VMEM((lats, lats), bf16),
            pltpu.VMEM((lats, LANES), f32),
            pltpu.VMEM((2 * LANES, 2 * LANES), bf16),
            pltpu.VMEM((2 * LANES, 2 * LANES), bf16),
            blocks,
            blocks,
            blocks,
            pltpu.VMEM((lats, 2 * LANES), bf16),
            pltpu.VMEM((lats, 2 * LANES), bf16),
            pltpu.VMEM((padded, 2 * LANES), bf16),
            pltpu.VMEM((2 * LANES, padded), bf16),
            pltpu.VMEM((2 * LANES, lats), bf16),
            blocks,
            blocks,
            blocks,
            dma2,
            pltpu.SemaphoreType.DMA,
        ]
        + [dma2] * 6
        + [pltpu.SemaphoreType.DMA((2, 4))] * 2
        + [dma2],
        compiler_params=pltpu.CompilerParams(
            collective_id=0, has_side_effects=True, vmem_limit_bytes=56 << 20
        ),
        cost_estimate=pl.CostEstimate(
            flops=flops, bytes_accessed=slots * lats * 4, transcendentals=0
        ),
        name="spectral_step",
    )(
        window_waves,
        fourier.reshape(8 * n, 2 * LANES),
        legendre[0, 0],
        lat_order.reshape(lats // LANES, LANES),
        gauss_weights.reshape(lats // LANES, LANES),
        mode_rates.reshape(1, LANES),
        mode_in,
        mode_out,
    )
    rows = pl.pallas_call(
        functools.partial(row_kernel, n),
        out_shape=jax.ShapeDtypeStruct((8 * n, 2 * LANES), f32),
        in_specs=[vmem],
        out_specs=vmem,
        name="latitude_rows",
    )(out.reshape(2, 8 * n, LANES))
    return rows.reshape(1, 8, n, 2 * LANES)


def solution(mesh):
    return jax.shard_map(
        per_device,
        mesh=mesh,
        in_specs=(
            P("par", "wave", None, None),
            P("wave", "par", None, None),
            P("wave"),
            P(),
            P(),
            P(),
            P(),
            P(),
        ),
        out_specs=P("par", "wave", None, None),
        check_vma=False,
    )
```

```python
import functools

import jax
import jax.numpy as jnp
from jax import lax
from jax.experimental import pallas as pl
from jax.experimental.pallas import tpu as pltpu
from jax.sharding import PartitionSpec as P

TRUNC = 3999
LANES = 128
MESH = pl.DeviceIdType.MESH
f32, bf16 = jnp.float32, jnp.bfloat16


def each_peer(me, n, visit):
    group, z = lax.div(me, 8), lax.rem(me, 8)
    near = [z] + [lax.rem(z + dz, 8) for dz in range(1, 8)]
    for dz in range(1, 8):
        visit(group * 8 + near[dz])

    @pl.loop(1, n // 8)
    def _(g):
        if n == 128:
            x, y = lax.div(group, 4), lax.rem(group, 4)
            there = lax.rem(x + lax.div(g, 4), 4) * 4 + lax.rem(y + lax.rem(g, 4), 4)
        else:
            there = lax.rem(group + g, n // 8)
        for dz in range(8):
            visit(there * 8 + near[dz])


def split(value):
    high = value.astype(bf16)
    return high, (value - high.astype(f32)).astype(bf16)


def mm(a, b):
    return jnp.dot(a, b, preferred_element_type=f32)


def mm_nt(a, b):
    return lax.dot_general(a, b, (((1,), (1,)), ((), ())), preferred_element_type=f32)


def step_kernel(
    n, wave_ref, field_hbm, table_hbm, order_ref, gauss_ref, rates_ref, in_ref, out_mat_ref,
    result,
    field, table, high, low, pick, place, gauss_col, in_terms, out_terms,
    send, recv, other, stack, weighted, terms, solved_t, grid_t, back, back_other, send_out,
    field_sem, table_sem, in_send, in_recv, pair_send, pair_recv,
    out_send, out_recv, back_send, back_recv, own_sem,
):
    me = lax.axis_index("wave")
    par = lax.axis_index("par")
    lats = 8 * n
    slots = table.shape[0]
    padded = high.shape[0]
    tile = min(256, lats)
    jtile, vtile, ctile, ltile = min(1024, padded), min(1024, padded), min(512, lats), min(1024, lats)
    sign = (1 - 2 * par).astype(f32)
    partner = {"par": 1 - par}

    barrier = pltpu.get_barrier_semaphore()
    field_in = [
        pltpu.make_async_copy(
            field_hbm.at[:, pl.ds(h * LANES, LANES)], field.at[h], field_sem.at[h]
        )
        for h in range(2)
    ]
    for copy in field_in:
        copy.start()
    table_in = pltpu.make_async_copy(table_hbm, table, table_sem)
    table_in.start()
    pl.semaphore_signal(barrier, inc=1, device_id=partner, device_id_type=MESH)

    def greet(d):
        pl.semaphore_signal(barrier, inc=1, device_id={"wave": d}, device_id_type=MESH)

    each_peer(me, n, greet)

    for h in range(2):
        field_in[h].wait()

        @pl.loop(0, n, unroll=8)
        def _(w, h=h):
            send[h, w] = field[h, pl.ds(w, 8, stride=n), :]

        recv[h, pl.ds(me, 1)] = send[h, pl.ds(me, 1)]

    pl.semaphore_wait(barrier, n)

    def send_all(source, target, send_sem, recv_sem, h):
        def send_to(d):
            pltpu.make_async_remote_copy(
                src_ref=source.at[h, d],
                dst_ref=target.at[h, me],
                send_sem=send_sem.at[h],
                recv_sem=recv_sem.at[h],
                device_id={"wave": d},
                device_id_type=MESH,
            ).start()

        each_peer(me, n, send_to)

    def all_of(source, target, send_sem, recv_sem, h):
        return pltpu.make_async_remote_copy(
            src_ref=source.at[h, pl.ds(0, n - 1)],
            dst_ref=target.at[h, pl.ds(0, n - 1)],
            send_sem=send_sem.at[h],
            recv_sem=recv_sem.at[h],
            device_id=partner,
            device_id_type=MESH,
        )

    send_all(send, recv, in_send, in_recv, 0)

    for t in range(lats // LANES):
        rows = pl.ds(t * LANES, LANES)
        gauss_col[rows, :] = jnp.broadcast_to(gauss_ref[t : t + 1, :], (LANES, LANES)).T
        order_t = jnp.broadcast_to(order_ref[t : t + 1, :].astype(f32), (LANES, LANES)).T
        order_t = order_t.astype(jnp.int32)
        for c in range(lats // LANES):
            lat = lax.broadcasted_iota(jnp.int32, (LANES, LANES), 1) + c * LANES
            pick[rows, pl.ds(c * LANES, LANES)] = jnp.where(order_t == lat, 1.0, 0.0).astype(bf16)

    @pl.loop(0, lats // LANES)
    def _(c):
        lat = lax.broadcasted_iota(jnp.int32, (LANES, LANES), 0) + c * LANES
        for t in range(lats // LANES):
            same = order_ref[t : t + 1, :] == lat
            place[pl.ds(pl.multiple_of(c * LANES, LANES), LANES), pl.ds(t * LANES, LANES)] = (
                jnp.where(same, 1.0, 0.0).astype(bf16)
            )

    in_high, in_low = split(in_ref[...])
    in_terms[:LANES, :LANES], in_terms[:LANES, LANES:] = in_high, in_low
    in_terms[LANES:, :LANES], in_terms[LANES:, LANES:] = in_high, jnp.zeros_like(in_low)
    out_high, out_low = split(out_mat_ref[...].T)
    out_terms[:LANES, :LANES], out_terms[:LANES, LANES:] = out_high, out_high
    out_terms[LANES:, :LANES], out_terms[LANES:, LANES:] = out_low, jnp.zeros_like(out_low)
    table_in.wait()

    @pl.loop(0, slots // 16)
    def _(c):
        rows = pl.ds(pl.multiple_of(c * 16, 16), 16)
        high[rows, :], low[rows, :] = split(table[rows, :])

    rest = padded - slots
    high[pl.ds(slots, rest), :] = jnp.zeros((rest, lats), bf16)
    low[pl.ds(slots, rest), :] = jnp.zeros((rest, lats), bf16)

    def pair_of(h):
        return pltpu.make_async_remote_copy(
            src_ref=recv.at[h], dst_ref=other.at[h], send_sem=pair_send.at[h],
            recv_sem=pair_recv.at[h], device_id=partner, device_id_type=MESH,
        )

    def swap_of(h, t):
        blocks = pl.ds(t * (tile // 8), tile // 8)
        return pltpu.make_async_remote_copy(
            src_ref=back.at[h, blocks], dst_ref=back_other.at[h, blocks],
            send_sem=back_send.at[h, t], recv_sem=back_recv.at[h, t],
            device_id=partner, device_id_type=MESH,
        )

    def solve(h):
        @pl.loop(0, lats // tile)
        def _(t):
            blocks = pl.ds(t * (tile // 8), tile // 8)
            paired = other[h, blocks] + sign * recv[h, blocks]
            rows = pl.ds(pl.multiple_of(t * tile, tile), tile)
            stack[rows, :LANES], stack[rows, LANES:] = split(paired.reshape(tile, LANES))

        for t in range(lats // ltile):
            rows = pl.ds(t * ltile, ltile)
            both = mm(place[rows, :], stack[...])
            scaled = (both[:, :LANES] + both[:, LANES:]) * gauss_col[rows, :]
            weighted[rows, :LANES], weighted[rows, LANES:] = split(scaled)

        @pl.loop(0, padded // jtile)
        def _(t):
            rows = pl.ds(pl.multiple_of(t * jtile, jtile), jtile)
            both = mm(high[rows, :], weighted[...])
            summed = both[:, :LANES] + both[:, LANES:] + mm(low[rows, :], weighted[:, :LANES])
            slot = lax.broadcasted_iota(jnp.int32, (jtile, LANES), 0) + t * jtile
            degree = wave_ref[0] + par + 2 * slot
            spectrum = jnp.where(degree <= TRUNC, summed, 0.0)
            terms[rows, :LANES], terms[rows, LANES:] = split(spectrum)

        @pl.loop(0, padded // vtile)
        def _(t):
            rows = pl.ds(pl.multiple_of(t * vtile, vtile), vtile)
            slot = lax.broadcasted_iota(jnp.int32, (vtile, LANES), 0) + t * vtile
            degree = (wave_ref[0] + par + 2 * slot).astype(f32)
            both = mm(terms[rows, :], in_terms[...])
            scale = degree * (degree + 1.0) / (TRUNC * (TRUNC + 1.0))
            modes = (both[:, :LANES] + both[:, LANES:]) / (1.0 + scale * rates_ref[...])
            modes = jnp.concatenate(split(modes), axis=1)
            both = mm_nt(out_terms[...], modes)
            solved_t[:LANES, rows], solved_t[LANES:, rows] = split(both[:LANES] + both[LANES:])

        @pl.loop(0, lats // ctile)
        def _(t):
            cols = pl.ds(pl.multiple_of(t * ctile, ctile), ctile)
            both = mm(solved_t[...], high[:, cols])
            grid = both[:LANES] + both[LANES:] + mm(solved_t[:LANES, :], low[:, cols])
            grid_t[:LANES, cols], grid_t[LANES:, cols] = split(grid)

        for t in range(lats // tile):
            both = mm_nt(pick[pl.ds(t * tile, tile), :], grid_t[...])
            back[h, pl.ds(t * (tile // 8), tile // 8)] = (
                both[:, :LANES] + both[:, LANES:]
            ).reshape(tile // 8, 8, LANES)
            swap_of(h, t).start()

    def send_back(h):
        for t in range(lats // tile):
            swap_of(h, t).wait()
            blocks = pl.ds(t * (tile // 8), tile // 8)
            send_out[h, blocks] = back_other[h, blocks] + sign * back[h, blocks]
        send_all(send_out, result, out_send, out_recv, h)
        own_out(h).start()

    def own_out(h):
        return pltpu.make_async_copy(send_out.at[h, me], result.at[h, me], own_sem.at[h])

    send_all(send, recv, in_send, in_recv, 1)
    all_of(send, recv, in_send, in_recv, 0).wait_recv()
    pair_of(0).start()
    pair_of(0).wait()
    solve(0)
    all_of(send, recv, in_send, in_recv, 1).wait_recv()
    pair_of(1).start()
    send_back(0)
    pair_of(1).wait()
    solve(1)
    send_back(1)

    for h in range(2):
        own_out(h).wait()
        all_of(send, recv, in_send, in_recv, h).wait_send()
        all_of(send_out, result, out_send, out_recv, h).wait()


def row_kernel(n, columns_ref, rows_ref):
    for h in range(2):

        @pl.loop(0, n // 8, unroll=True)
        def _(t):
            for r in range(8):
                rows = columns_ref[h, pl.ds(t * 64 + r, 8, stride=8), :]
                rows_ref[pl.ds(r * n + t * 8, 8), pl.ds(h * LANES, LANES)] = rows


def per_device(
    fourier, legendre, window_waves, lat_order, gauss_weights, mode_rates, mode_in, mode_out
):
    n = lax.axis_size("wave")
    lats = gauss_weights.shape[0]
    slots = legendre.shape[2]
    padded = -(-slots // 256) * 256
    vmem = pl.BlockSpec(memory_space=pltpu.VMEM)
    anywhere = pl.BlockSpec(memory_space=pl.ANY)
    blocks = pltpu.VMEM((2, n, 8, LANES), f32)
    dma2 = pltpu.SemaphoreType.DMA((2,))
    flops = 24 * slots * lats * LANES
    out = pl.pallas_call(
        functools.partial(step_kernel, n),
        out_shape=jax.ShapeDtypeStruct((2, n, 8, LANES), f32),
        in_specs=[pl.BlockSpec(memory_space=pltpu.SMEM), anywhere, anywhere] + [vmem] * 5,
        out_specs=anywhere,
        scratch_shapes=[
            pltpu.VMEM((2, lats, LANES), f32),
            pltpu.VMEM((slots, lats), f32),
            pltpu.VMEM((padded, lats), bf16),
            pltpu.VMEM((padded, lats), bf16),
            pltpu.VMEM((lats, lats), bf16),
            pltpu.VMEM((lats, lats), bf16),
            pltpu.VMEM((lats, LANES), f32),
            pltpu.VMEM((2 * LANES, 2 * LANES), bf16),
            pltpu.VMEM((2 * LANES, 2 * LANES), bf16),
            blocks,
            blocks,
            blocks,
            pltpu.VMEM((lats, 2 * LANES), bf16),
            pltpu.VMEM((lats, 2 * LANES), bf16),
            pltpu.VMEM((padded, 2 * LANES), bf16),
            pltpu.VMEM((2 * LANES, padded), bf16),
            pltpu.VMEM((2 * LANES, lats), bf16),
            blocks,
            blocks,
            blocks,
            dma2,
            pltpu.SemaphoreType.DMA,
        ]
        + [dma2] * 6
        + [pltpu.SemaphoreType.DMA((2, 4))] * 2
        + [dma2],
        compiler_params=pltpu.CompilerParams(
            collective_id=0, has_side_effects=True, vmem_limit_bytes=56 << 20
        ),
        cost_estimate=pl.CostEstimate(
            flops=flops, bytes_accessed=slots * lats * 4, transcendentals=0
        ),
        name="spectral_step",
    )(
        window_waves,
        fourier.reshape(8 * n, 2 * LANES),
        legendre[0, 0],
        lat_order.reshape(lats // LANES, LANES),
        gauss_weights.reshape(lats // LANES, LANES),
        mode_rates.reshape(1, LANES),
        mode_in,
        mode_out,
    )
    rows = pl.pallas_call(
        functools.partial(row_kernel, n),
        out_shape=jax.ShapeDtypeStruct((8 * n, 2 * LANES), f32),
        in_specs=[vmem],
        out_specs=vmem,
        name="latitude_rows",
    )(out.reshape(2, 8 * n, LANES))
    return rows.reshape(1, 8, n, 2 * LANES)


def solution(mesh):
    return jax.shard_map(
        per_device,
        mesh=mesh,
        in_specs=(
            P("par", "wave", None, None),
            P("wave", "par", None, None),
            P("wave"),
            P(),
            P(),
            P(),
            P(),
            P(),
        ),
        out_specs=P("par", "wave", None, None),
        check_vma=False,
    )
```
